512 devices in a mesh: batch: 32 (over y_lo, z), seq: 16 (over y_hi, x, core).
Axes of the slice: x: 4, y: 8 (y_hi: 2, y_lo: 4; y = y_hi * 4 + y_lo), z: 8, core: 2. Of those that a mesh axis runs over, the one named last changes fastest.
Arguments:
- sequence_input: bfloat16 [32, 4096, 768], P('batch', 'seq'), may hold values from -64 to 64
- bn_gain: float32 [768], replicated, may hold values from 0.1 to 1.9
- bn_bias: float32 [768], replicated, may hold values from -3 to 3
- conv_weight: bfloat16 [5, 768, 768], P(None, None, 'batch'), may hold values from -0.09375 to 0.09375
- conv_bias: float32 [768], replicated, may hold values from -3 to 3
- ln_gain: float32 [768], replicated, may hold values from 0.1 to 1.9
- ln_bias: float32 [768], replicated, may hold values from -3 to 3
- qkv_weight: bfloat16 [768, 1792], P(None, 'batch'), may hold values from -32 to 32
Outputs:
- pooled: bfloat16 [32, 2048, 768], P('batch', 'seq')
- attended: bfloat16 [32, 2048, 768], P('batch', 'seq')
The draws below stay inside these ranges and needn't reach their ends.
All inputs are finite; a program needn't handle non-finite values.
Results may differ from the reference program's by a relative error of at most 0.025.
The reference program's roundings to bfloat16 on the way (of `activated`, `normed`, `queries` and `weights`) count: a program that leaves them out, or rounds other values in their place, can miss the bound.
Values may be sent and summed in bfloat16 or wider, within the bound.
No kernel may reach another device: no remote copies, remote signals or barrier semaphores. Data moves between devices by JAX's collectives and lax.ppermute only.
A program may use at most 64 MiB of HBM per device.

```python
import jax
import jax.numpy as jnp
from jax import lax

D = 768
HEADS = 8
KEY = 64
VAL = 96
KW = 5
RAW = 4096
BATCH = 32


def draw_sequence_input(key, part):
    base = jax.random.fold_in(key, 101)
    keys_list = jax.random.split(base, 4)
    chan_scale = jnp.exp(jax.random.uniform(keys_list[0], (D,), jnp.float32, jnp.log(0.3), jnp.log(3.0)))
    chan_mean = 0.7 * jax.random.normal(keys_list[1], (D,), jnp.float32)
    place = jnp.arange(RAW, dtype=jnp.float32) / RAW
    row_scale = 10.0 ** (place - 0.5)
    seq_place = jnp.arange(BATCH, dtype=jnp.float32) / max(BATCH - 1, 1)
    seq_scale = 3.0 ** (seq_place - 0.5)
    rough = jnp.exp(jax.random.uniform(keys_list[2], (BATCH, RAW, 1), jnp.float32, -0.35, 0.35))
    noise = jax.random.normal(keys_list[3], (BATCH, RAW, D), jnp.float32)
    values_out = (noise * chan_scale + chan_mean) * rough * row_scale[None, :, None] * seq_scale[:, None, None]
    return jnp.clip(values_out, -64.0, 64.0).astype(jnp.bfloat16)


def draw_qkv_weight(key, part):
    base = jax.random.fold_in(key, 202)
    keys_list = jax.random.split(base, 3)
    factor = D ** (-0.5)
    query_part = jax.random.normal(keys_list[0], (D, HEADS * KEY), jnp.float32) * factor
    key_part = jax.random.normal(keys_list[1], (D, HEADS * KEY), jnp.float32) * factor
    value_part = jax.random.normal(keys_list[2], (D, HEADS * VAL), jnp.float32) * factor
    query_part = 2.5 * query_part
    joined = jnp.concatenate([query_part, key_part, value_part], axis=1)
    return jnp.clip(joined, -32.0, 32.0).astype(jnp.bfloat16)


def block_scale(rng, dims, shards, low, top_value):
    factor_of = 1.0
    for axis_at, shards_of in shards:
        draws = jax.random.uniform(jax.random.fold_in(jax.random.fold_in(rng, 6), axis_at), (shards_of,), jnp.float32, low / len(shards), top_value / len(shards))
        factor_of = factor_of * jnp.repeat(jnp.exp(draws), dims[axis_at] // shards_of).reshape((-1,) + (1,) * (len(dims) - 1 - axis_at))
    return factor_of


def scatter_about(stream_key, dims, scale, reach, cuts=(), kind=jnp.bfloat16):
    level = block_scale(stream_key, dims, cuts, -0.22, 0.18) if cuts else 1.0
    values = jax.random.normal(stream_key, dims, jnp.float32) * scale * level
    return jnp.minimum(jnp.maximum(values, -reach), reach).astype(kind)


def setup_inputs(seed: int = 0) -> dict:
    streams_of = jax.random.split(jax.random.key(seed), 9)
    sequence_input = draw_sequence_input(jax.random.fold_in(streams_of[8], 71), 0)
    bn_gain = jnp.clip(1.0 + 0.18 * jax.random.normal(streams_of[1], (D,), jnp.float32), 0.1, 1.9)
    bn_bias = scatter_about(streams_of[2], (D,), 0.5, 3.0, (), jnp.float32)
    conv_weight = scatter_about(streams_of[3], (KW, D, D), (KW * D) ** -0.5, 0.09375, ((2, 32),))
    conv_bias = scatter_about(streams_of[4], (D,), 0.5, 3.0, (), jnp.float32)
    ln_gain = jnp.clip(1.0 + 0.18 * jax.random.normal(streams_of[5], (D,), jnp.float32), 0.1, 1.9)
    ln_bias = scatter_about(streams_of[6], (D,), 0.5, 3.0, (), jnp.float32)
    qkv_weight = draw_qkv_weight(jax.random.fold_in(streams_of[8], 71), 0)
    return {"sequence_input": sequence_input, "bn_gain": bn_gain, "bn_bias": bn_bias, "conv_weight": conv_weight, "conv_bias": conv_bias, "ln_gain": ln_gain, "ln_bias": ln_bias, "qkv_weight": qkv_weight}


epsilon = 1e-05

def reference(sequence_input, bn_gain, bn_bias, conv_weight, conv_bias, ln_gain, ln_bias, qkv_weight):
    whole = sequence_input.astype(jnp.float32)
    count = whole.shape[0] * whole.shape[1]
    total = lax.optimization_barrier(jnp.sum(whole, axis=(0, 1)))
    squares = lax.optimization_barrier(jnp.sum(whole * whole, axis=(0, 1)))
    mean = total / count
    var = squares / count - mean * mean
    head_keys = HEADS * KEY

    def one_sequence(single):
        values_in = single.astype(jnp.float32)
        activated = jax.nn.gelu((values_in - mean) * lax.rsqrt(var + epsilon) * bn_gain + bn_bias, approximate=True).astype(jnp.bfloat16)
        positions = activated.shape[0]
        padded = jnp.pad(activated, ((2, 2), (0, 0)))
        conv_out = jnp.zeros((positions, conv_weight.shape[2]), jnp.float32) + conv_bias
        for tap_index in range(conv_weight.shape[0]):
            conv_out = conv_out + jnp.dot(padded[tap_index:tap_index + positions], conv_weight[tap_index], preferred_element_type=jnp.float32)
        pooled = conv_out.reshape(positions // 2, 2, conv_out.shape[1]).max(axis=1).astype(jnp.bfloat16)
        pooled_wide = pooled.astype(jnp.float32)
        centre = lax.optimization_barrier(jnp.mean(pooled_wide, axis=-1, keepdims=True))
        spread = lax.optimization_barrier(jnp.mean((pooled_wide - centre) ** 2, axis=-1, keepdims=True))
        normed = ((pooled_wide - centre) * lax.rsqrt(spread + epsilon) * ln_gain + ln_bias).astype(jnp.bfloat16)
        proj = jnp.dot(normed, qkv_weight, preferred_element_type=jnp.float32)
        bins = proj.shape[0]
        queries = (proj[:, :head_keys] * KEY ** (-0.5)).astype(jnp.bfloat16)
        key_rows = proj[:, head_keys:2 * head_keys].astype(jnp.bfloat16)
        value_rows = proj[:, 2 * head_keys:].astype(jnp.bfloat16)
        queries, key_rows, value_rows = lax.optimization_barrier((queries, key_rows, value_rows))
        query_wide = queries.astype(jnp.float32).reshape(bins, HEADS, KEY)
        key_wide = key_rows.astype(jnp.float32).reshape(bins, HEADS, KEY)
        value_wide = value_rows.astype(jnp.float32).reshape(bins, HEADS, VAL)
        scores = jnp.einsum('qhk,jhk->hqj', query_wide, key_wide)
        largest = lax.optimization_barrier(jnp.max(scores, axis=-1, keepdims=True))
        exps = jnp.exp(scores - largest)
        denominator = lax.optimization_barrier(jnp.sum(exps, axis=-1))
        weights = lax.optimization_barrier(exps.astype(jnp.bfloat16)).astype(jnp.float32)
        summed = jnp.einsum('hqj,jhv->hqv', weights, value_wide)
        attended = (summed / denominator[..., None]).transpose(1, 0, 2).reshape(bins, HEADS * VAL).astype(jnp.bfloat16)
        return (pooled, attended)
    pooled, attended = lax.map(one_sequence, sequence_input)
    return (pooled, attended)
```

```python
import functools

import jax
import jax.numpy as jnp
from jax import lax
from jax.experimental import pallas as pl
from jax.experimental.pallas import tpu as pltpu
from jax.sharding import PartitionSpec as P

HEADS = 8
KEY = 64
VAL = 96
epsilon = 1e-05

Y_LO, Z = 4, 8
Z_GROUPS = [[y * Z + z for z in range(Z)] for y in range(Y_LO)]
Y_GROUPS = [[y * Z + z for y in range(Y_LO)] for z in range(Z)]


def y_shift(step):
    pairs = []
    for batch in range(Y_LO * Z):
        for seq in range(16):
            y_lo, z = divmod(batch, Z)
            y_hi, rest = divmod(seq, 8)
            y = (y_hi * Y_LO + y_lo + step) % (2 * Y_LO)
            target = ((y % Y_LO) * Z + z) * 16 + (y // Y_LO) * 8 + rest
            pairs.append((batch * 16 + seq, target))
    return pairs


def y_lo_shift(step):
    return [(i, (i // Z + step) % Y_LO * Z + i % Z) for i in range(Y_LO * Z)]


def to_all(values, axis, groups=None):
    count = len(groups[0]) if groups else lax.axis_size(axis)
    return lax.all_to_all(
        jnp.broadcast_to(values[None], (count,) + values.shape),
        axis, 0, 0, axis_index_groups=groups, tiled=True,
    )


def attend_kernel(half_ref, r_ref, o_ref):
    first = half_ref[0] * 64
    keys = r_ref[:, :, :64].reshape(2048, KEY)
    values = r_ref[:, :, 128:224].reshape(2048, VAL)
    for i in range(4):
        q = r_ref[i * 4 : (i + 1) * 4, pl.ds(pl.multiple_of(first, 64), 64), 64:128]
        q = q.reshape(256, KEY)
        scores = lax.dot_general(
            q, keys, (((1,), (1,)), ((), ())), preferred_element_type=jnp.float32
        )
        exps = jnp.exp(scores - jnp.max(scores, axis=-1, keepdims=True))
        total = jnp.sum(exps, axis=-1, keepdims=True)
        out = jnp.dot(exps.astype(jnp.bfloat16), values, preferred_element_type=jnp.float32)
        out = (out / total).astype(jnp.bfloat16).reshape(4, 64, VAL)
        o_ref[i * 4 : (i + 1) * 4, :, :VAL] = out
        o_ref[i * 4 : (i + 1) * 4, :, VAL:] = jnp.zeros((4, 64, 128 - VAL), jnp.bfloat16)


def attend(half, received):
    return pl.pallas_call(
        attend_kernel,
        out_shape=jax.ShapeDtypeStruct((16, 64, 128), jnp.bfloat16),
        in_specs=[
            pl.BlockSpec(memory_space=pltpu.SMEM),
            pl.BlockSpec(memory_space=pltpu.VMEM),
        ],
        out_specs=pl.BlockSpec(memory_space=pltpu.VMEM),
        compiler_params=pltpu.CompilerParams(vmem_limit_bytes=40 << 20),
        name="attend",
    )(half, received)


def on_device(
    sequence_input, bn_gain, bn_bias, conv_weight, conv_bias, ln_gain, ln_bias, qkv_weight
):
    raw = sequence_input[0]
    channels = raw.shape[1]
    y_lo = lax.axis_index("batch") // Z
    seq = lax.axis_index("seq")
    core = seq % 2
    rel = (y_lo - jnp.arange(Y_LO)) % Y_LO

    both = jnp.concatenate(
        [conv_weight.transpose(0, 2, 1).reshape(120, channels), qkv_weight.T], axis=0
    )
    mine = lax.dynamic_slice(both, (0, core * 384), (176, 384))
    gathered = lax.all_gather(mine, "batch", axis=0, axis_index_groups=Z_GROUPS)
    swap = [(i, i ^ 1) for i in range(16)]
    conv_mine = gathered[:, :120]
    conv_other = lax.ppermute(conv_mine, "seq", swap)
    qkv_mine = gathered[:, 120:].reshape(448, 384)
    qkv_blocks = [qkv_mine] + [
        lax.ppermute(qkv_mine, ("batch", "seq"), y_shift(step)) for step in (1, 2, -1)
    ]
    qkv_mine = jnp.take(jnp.stack(qkv_blocks), rel, axis=0).reshape(1792, 384)
    qkv_other = lax.ppermute(qkv_mine, "seq", swap)

    def joined(own, other):
        low = jnp.where(core == 0, own, other)
        high = jnp.where(core == 0, other, own)
        return jnp.concatenate([low, high], axis=-1)

    blocks = jnp.stack(
        [raw] + [lax.ppermute(raw, "batch", y_lo_shift(k)) for k in range(1, Y_LO)]
    )

    wide = raw.astype(jnp.float32)
    sums = jnp.stack([jnp.sum(wide, axis=0), jnp.sum(wide * wide, axis=0)])
    edges = jnp.concatenate([wide[:2], wide[-2:]], axis=0)
    first = to_all(jnp.concatenate([sums, edges], axis=0), "seq")
    sums = jnp.sum(first[:, :2], axis=0)
    left = lax.dynamic_index_in_dim(first, jnp.maximum(seq - 1, 0), 0, keepdims=False)[4:6]
    right = lax.dynamic_index_in_dim(first, jnp.minimum(seq + 1, 15), 0, keepdims=False)[2:4]
    sums = jnp.sum(to_all(sums, "batch", Z_GROUPS), axis=0)
    third = to_all(jnp.concatenate([sums, left, right], axis=0), "batch", Y_GROUPS)
    sums = jnp.sum(third[:, :2], axis=0)
    halos = jnp.take(third[:, 2:], rel, axis=0)
    count = float(raw.shape[0] * lax.axis_size("batch") * lax.axis_size("seq"))
    mean = sums[0] / count
    var = sums[1] / count - mean * mean

    def activate(values):
        return jax.nn.gelu(
            (values - mean) * lax.rsqrt(var + epsilon) * bn_gain + bn_bias, approximate=True
        ).astype(jnp.bfloat16)

    left = jnp.where(seq > 0, activate(halos[:, :2]), 0)
    right = jnp.where(seq < 15, activate(halos[:, 2:]), 0)
    rows = jnp.concatenate([left, activate(blocks.astype(jnp.float32)), right], axis=1)

    kernel = joined(conv_mine, conv_other).reshape(Z, 5, 24, channels)
    kernel = kernel.transpose(1, 0, 2, 3).reshape(5, 192, channels)
    conv = None
    for tap in range(5):
        product = jnp.einsum(
            "kpc,oc->kpo", rows[:, tap : tap + 256], kernel[tap],
            preferred_element_type=jnp.float32,
        )
        conv = product if conv is None else conv + product
    conv = conv + lax.dynamic_slice(conv_bias, (y_lo * 192,), (192,))
    part = conv.reshape(Y_LO, 128, 2, 192).max(axis=2).astype(jnp.bfloat16)
    part = lax.all_to_all(
        jnp.take(part, rel, axis=0), "batch", 0, 0, axis_index_groups=Y_GROUPS, tiled=True
    )
    pooled = part.transpose(1, 0, 2).reshape(128, channels)

    pooled_wide = pooled.astype(jnp.float32)
    centre = jnp.mean(pooled_wide, axis=-1, keepdims=True)
    spread = jnp.mean((pooled_wide - centre) ** 2, axis=-1, keepdims=True)
    normed = ((pooled_wide - centre) * lax.rsqrt(spread + epsilon) * ln_gain + ln_bias).astype(
        jnp.bfloat16
    )
    proj = jnp.einsum(
        "bd,kd->bk", normed, joined(qkv_mine, qkv_other), preferred_element_type=jnp.float32
    )
    queries = (proj[:, :512] * KEY ** (-0.5)).astype(jnp.bfloat16).reshape(128, HEADS, KEY)
    keys = proj[:, 512:1024].astype(jnp.bfloat16).reshape(128, HEADS, KEY)
    values = proj[:, 1024:].astype(jnp.bfloat16).reshape(128, HEADS, VAL)
    pad = jnp.zeros((128, HEADS, 32), jnp.bfloat16)
    packed = jnp.concatenate([keys, queries, values, pad], axis=-1).transpose(1, 0, 2)
    packed = jnp.broadcast_to(packed[None], (2,) + packed.shape).reshape(16, 128, 256)
    received = lax.all_to_all(packed, "seq", 0, 0, tiled=True)
    out = attend((seq // 8).astype(jnp.int32)[None], received)
    out = lax.all_to_all(out, "seq", 0, 0, tiled=True)[..., :VAL]
    attended = out.reshape(2, HEADS, 64, VAL).transpose(0, 2, 1, 3).reshape(128, HEADS * VAL)
    return (pooled[None], attended[None])


def solution(mesh):
    placed = (
        P("batch", "seq", None),
        P(),
        P(),
        P(None, None, "batch"),
        P(),
        P(),
        P(),
        P(None, "batch"),
    )
    return jax.shard_map(
        on_device,
        mesh=mesh,
        in_specs=placed,
        out_specs=(P("batch", "seq", None), P("batch", "seq", None)),
        check_vma=False,
    )
```

```python
import functools

import jax
import jax.numpy as jnp
from jax import lax
from jax.experimental import pallas as pl
from jax.experimental.pallas import tpu as pltpu
from jax.sharding import PartitionSpec as P

HEADS = 8
KEY = 64
VAL = 96
ROWS = 2 * KEY + VAL
epsilon = 1e-05

Y_LO, Z = 4, 8
Z_GROUPS = [[y * Z + z for z in range(Z)] for y in range(Y_LO)]
X_GROUPS = [[half * 8 + x * 2 + core for x in range(4)] for half in range(2) for core in range(2)]
HALF_GROUPS = [list(range(8)), list(range(8, 16))]


def x_shift(step):
    return [(i, i // 8 * 8 + (i // 2 + step) % 4 * 2 + i % 2) for i in range(16)]


def quarters():
    pairs = []
    for batch in range(Y_LO * Z):
        for seq in range(16):
            y_lo, z = divmod(batch, Z)
            y_hi, x = seq // 8, seq // 2 % 4
            source = (y_hi * Y_LO + y_lo + (0, 1, 2, -1)[x]) % (2 * Y_LO)
            source_batch = source % Y_LO * Z + z
            pairs.append((source_batch * 16 + source // Y_LO * 8 + seq % 8, batch * 16 + seq))
    return pairs


def to_all(values, axis, groups=None):
    count = len(groups[0]) if groups else lax.axis_size(axis)
    return lax.all_to_all(
        jnp.broadcast_to(values[None], (count,) + values.shape),
        axis, 0, 0, axis_index_groups=groups, tiled=True,
    )


def qkv_rows(gathered):
    tiles = gathered[:, :, 1920:].reshape(Z, 3, 8, 7, 128)
    return tiles.transpose(0, 3, 2, 1, 4).reshape(448, 384)


def attend_kernel(first_ref, r_ref, o_ref):
    keys = jnp.concatenate([r_ref[j, KEY : 2 * KEY, :] for j in range(16)], axis=1).T
    values = jnp.concatenate([r_ref[j, 2 * KEY :, :] for j in range(16)], axis=1)
    first = first_ref[0]
    for i in range(0, 8, 2):
        q = jnp.concatenate([r_ref[first + i, :KEY, :], r_ref[first + i + 1, :KEY, :]], axis=1)
        scores = jnp.dot(keys, q, preferred_element_type=jnp.float32)
        exps = jnp.exp(scores - jnp.max(scores, axis=0, keepdims=True))
        total = jnp.sum(exps, axis=0, keepdims=True)
        out = jnp.dot(values, exps.astype(jnp.bfloat16), preferred_element_type=jnp.float32)
        out = (out / total).astype(jnp.bfloat16)
        o_ref[i] = out[:, :128]
        o_ref[i + 1] = out[:, 128:]


def attend(first, received):
    return pl.pallas_call(
        attend_kernel,
        out_shape=jax.ShapeDtypeStruct((8, VAL, 128), jnp.bfloat16),
        in_specs=[
            pl.BlockSpec(memory_space=pltpu.SMEM),
            pl.BlockSpec(memory_space=pltpu.VMEM),
        ],
        out_specs=pl.BlockSpec(memory_space=pltpu.VMEM),
        compiler_params=pltpu.CompilerParams(vmem_limit_bytes=20 << 20),
        name="attend",
    )(first, received)


def conv_kernel(where_ref, x0, x1, x2, x3, sums_ref, norm_ref, mine_ref, other_ref, bias_ref,
                out_ref, act, product, held, arrived, *, count):
    core, x_at, y_hi = where_ref[0], where_ref[1], where_ref[2]
    mean = sums_ref[0:1] / count
    scale = lax.rsqrt(sums_ref[1:2] / count - mean * mean + epsilon) * norm_ref[0:1]
    shift = norm_ref[1:2]
    near = pl.multiple_of(core * 384, 128)
    far = pl.multiple_of(384 - core * 384, 128)

    def activated(values):
        return jax.nn.gelu(
            (values.astype(jnp.float32) - mean) * scale + shift, approximate=True
        ).astype(jnp.bfloat16)

    copies = [
        pltpu.make_async_copy(x_ref, held.at[k], arrived.at[k])
        for k, x_ref in enumerate((x0, x1, x2, x3))
    ]
    for copy in copies:
        copy.start()
    for k in range(4):
        copies[k].wait()
        slot = lax.rem(x_at + 4 - k, 4)
        seq = y_hi * 8 + slot * 2 + core
        edge = activated(held[k, 0:16])
        row = lax.broadcasted_iota(jnp.int32, edge.shape, 0)
        act[k, 0:16] = jnp.where((row >= 14) & (seq > 0), edge, jnp.zeros_like(edge))
        edge = activated(held[k, 272:288])
        act[k, 272:288] = jnp.where((row < 2) & (seq < 15), edge, jnp.zeros_like(edge))

        @pl.loop(1, 17)
        def _(i):
            rows = pl.ds(pl.multiple_of(i * 16, 16), 16)
            act[k, rows] = activated(held[k, rows])

        for tap in range(5):
            nt = (((1,), (1,)), ((), ()))
            both = lax.dot_general(
                act[k, :, pl.ds(near, 384)], mine_ref[:, tap * 384 : (tap + 1) * 384], nt, preferred_element_type=jnp.float32
            ) + lax.dot_general(
                act[k, :, pl.ds(far, 384)], other_ref[:, tap * 384 : (tap + 1) * 384], nt, preferred_element_type=jnp.float32
            )
            product[tap] = both[:, :128]
            product[5 + tap, :, :64] = both[:, 128:]
        for base, lanes in ((0, 128), (5, 64)):
            pair = []
            for odd in range(2):
                total = product[base, pl.ds(14 + odd, 128, stride=2), :]
                for tap in range(1, 5):
                    total = total + product[base + tap, pl.ds(14 + odd + tap, 128, stride=2), :]
                pair.append(total[:, :lanes])
            columns = slice(base // 5 * 128, base // 5 * 128 + lanes)
            pooled = jnp.maximum(pair[0], pair[1]) + bias_ref[:, columns]
            pooled = pooled.astype(jnp.bfloat16)
            if base == 0:
                out_ref[slot, :128] = pooled
            else:
                out_ref[slot, 128:, :64] = pooled[:64]
                out_ref[slot, 128:, 64:] = pooled[64:]


def conv_block(where, blocks, sums, norm, mine, other, bias, count):
    vmem = pl.BlockSpec(memory_space=pltpu.VMEM)
    return pl.pallas_call(
        functools.partial(conv_kernel, count=count),
        out_shape=jax.ShapeDtypeStruct((4, 192, 128), jnp.bfloat16),
        in_specs=[pl.BlockSpec(memory_space=pltpu.SMEM)]
        + [pl.BlockSpec(memory_space=pl.ANY)] * 4
        + [vmem] * 5,
        out_specs=vmem,
        scratch_shapes=[
            pltpu.VMEM((4, 288, 768), jnp.bfloat16),
            pltpu.VMEM((10, 288, 128), jnp.float32),
            pltpu.VMEM((4, 288, 768), jnp.bfloat16),
            pltpu.SemaphoreType.DMA((4,)),
        ],
        compiler_params=pltpu.CompilerParams(vmem_limit_bytes=14 << 20),
        name="conv_block",
    )(where, *blocks, sums, norm, mine, other, bias)


def project_kernel(where_ref, part_ref, norm_ref, *refs):
    weights, (pooled_ref, out_ref, normed, proj) = refs[:8], refs[8:]
    core, x_at, y_lo = where_ref[0], where_ref[1], where_ref[3]
    near = pl.multiple_of(core * 384, 128)
    far = pl.multiple_of(384 - core * 384, 128)
    pieces = []
    for i in range(4):
        piece = part_ref[lax.rem(i + 4 - y_lo, 4)]
        pieces.append(piece[:128])
        pieces.append(jnp.concatenate([piece[128:, :64], piece[128:, 64:]], axis=0))
    pooled = jnp.concatenate(pieces, axis=1)
    pooled_ref[...] = pooled
    wide = pooled.astype(jnp.float32)
    wide = wide - jnp.mean(wide, axis=-1, keepdims=True)
    spread = jnp.mean(wide * wide, axis=-1, keepdims=True)
    normed[...] = (wide * lax.rsqrt(spread + epsilon) * norm_ref[0:1] + norm_ref[1:2]).astype(
        jnp.bfloat16
    )
    nt = (((1,), (1,)), ((), ()))
    for k in range(4):
        rows = pl.ds(pl.multiple_of(lax.rem(x_at + y_lo + 4 - k, 4) * 448, 64), 448)
        proj[rows] = lax.dot_general(
            weights[2 * k][...], normed[:, pl.ds(near, 384)], nt,
            preferred_element_type=jnp.float32,
        ) + lax.dot_general(
            weights[2 * k + 1][...], normed[:, pl.ds(far, 384)], nt,
            preferred_element_type=jnp.float32,
        )
    for h in range(HEADS):
        q = (proj[h * KEY : (h + 1) * KEY] * KEY ** (-0.5)).astype(jnp.bfloat16)
        k = proj[512 + h * KEY : 512 + (h + 1) * KEY].astype(jnp.bfloat16)
        v = proj[1024 + h * VAL : 1024 + (h + 1) * VAL].astype(jnp.bfloat16)
        for d in (h, h + HEADS):
            out_ref[d, :KEY] = q
            out_ref[d, KEY : 2 * KEY] = k
            out_ref[d, 2 * KEY :] = v


def project(where, part, norm, weights):
    vmem = pl.BlockSpec(memory_space=pltpu.VMEM)
    return pl.pallas_call(
        project_kernel,
        out_shape=(
            jax.ShapeDtypeStruct((128, 768), jnp.bfloat16),
            jax.ShapeDtypeStruct((16, ROWS, 128), jnp.bfloat16),
        ),
        in_specs=[pl.BlockSpec(memory_space=pltpu.SMEM)] + [vmem] * 10,
        out_specs=(vmem, vmem),
        scratch_shapes=[
            pltpu.VMEM((128, 768), jnp.bfloat16),
            pltpu.VMEM((1792, 128), jnp.float32),
        ],
        compiler_params=pltpu.CompilerParams(vmem_limit_bytes=14 << 20),
        name="project",
    )(where, part, norm, *weights)


def on_device(
    sequence_input, bn_gain, bn_bias, conv_weight, conv_bias, ln_gain, ln_bias, qkv_weight
):
    raw = sequence_input[0]
    channels = raw.shape[1]
    y_lo = lax.axis_index("batch") // Z
    seq = lax.axis_index("seq")
    core, x_at = seq % 2, seq // 2 % 4
    where = jnp.stack([core, x_at, seq // 8, y_lo]).astype(jnp.int32)
    swap = [(i, i ^ 1) for i in range(16)]

    conv_half = lax.dynamic_slice(conv_weight.transpose(0, 2, 1), (0, 0, core * 384), (5, 24, 384))
    qkv_half = lax.dynamic_slice(qkv_weight.T, (0, core * 384), (56, 384))
    mine = jnp.concatenate(
        [
            conv_half.transpose(1, 0, 2).reshape(24, 1920),
            qkv_half.reshape(7, 8, 3, 128).transpose(2, 1, 0, 3).reshape(24, 896),
        ],
        axis=1,
    )
    mine = lax.ppermute(mine, ("batch", "seq"), quarters())

    pad = jnp.zeros((14, channels), raw.dtype)
    left = lax.ppermute(raw[-2:], "seq", [(i, i + 1) for i in range(15)])
    right = lax.ppermute(raw[:2], "seq", [(i + 1, i) for i in range(15)])
    block = jnp.concatenate([pad, left, raw, right, pad], axis=0)

    wide = raw.astype(jnp.float32)
    sums = jnp.stack([jnp.sum(wide, axis=0), jnp.sum(wide * wide, axis=0)])
    sums = jnp.sum(to_all(sums, "seq"), axis=0)
    sums, mine, block = lax.optimization_barrier((sums, mine, block))
    mine = to_all(mine, "batch", Z_GROUPS)
    blocks = [block] + [lax.ppermute(block, "seq", x_shift(k)) for k in range(1, 4)]
    sums, mine, blocks = lax.optimization_barrier((sums, mine, blocks))
    other = lax.ppermute(mine, "seq", swap)
    own = qkv_rows(mine)
    right, left = (lax.ppermute(own, "seq", x_shift(k)) for k in (1, 3))
    sums = jnp.sum(to_all(sums, "batch"), axis=0)
    sums, right, left = lax.optimization_barrier((sums, right, left))
    near = [right, lax.ppermute(right, "seq", x_shift(1)), left]
    count = float(raw.shape[0] * lax.axis_size("batch") * lax.axis_size("seq"))

    part = conv_block(
        where, blocks, sums, jnp.stack([bn_gain, bn_bias]), mine.reshape(192, 2816), other.reshape(192, 2816),
        lax.dynamic_slice(conv_bias, ((y_lo + x_at) % 4 * 192,), (192,))[None], count,
    )
    near, other = lax.optimization_barrier((part, near, other))[1:]
    weights = [own, qkv_rows(other)]
    for values in near:
        weights += [values, lax.ppermute(values, "seq", swap)]
    part = lax.all_to_all(part, "seq", 0, 0, axis_index_groups=X_GROUPS, tiled=True)
    pooled, packed = project(where, part, jnp.stack([ln_gain, ln_bias]), weights)
    packed = lax.all_to_all(packed, "seq", 0, 0, tiled=True)
    out = attend((seq // 8 * 8).astype(jnp.int32)[None], packed)
    out = lax.all_to_all(out, "seq", 0, 0, axis_index_groups=HALF_GROUPS, tiled=True)
    attended = out.reshape(HEADS * VAL, 128).T
    return (pooled[None], attended[None])


def solution(mesh):
    placed = (
        P("batch", "seq", None),
        P(),
        P(),
        P(None, None, "batch"),
        P(),
        P(),
        P(),
        P(None, "batch"),
    )
    return jax.shard_map(
        on_device,
        mesh=mesh,
        in_specs=placed,
        out_specs=(P("batch", "seq", None), P("batch", "seq", None)),
        check_vma=False,
    )
```

```python
import functools

import jax
import jax.numpy as jnp
from jax import lax
from jax.experimental import pallas as pl
from jax.experimental.pallas import tpu as pltpu
from jax.sharding import PartitionSpec as P

HEADS = 8
KEY = 64
VAL = 96
ROWS = 2 * KEY + VAL
epsilon = 1e-05

Y_LO, Z = 4, 8
Z_GROUPS = [[y * Z + z for z in range(Z)] for y in range(Y_LO)]
X_GROUPS = [[half * 8 + x * 2 + core for x in range(4)] for half in range(2) for core in range(2)]
HALF_GROUPS = [list(range(8)), list(range(8, 16))]


def x_shift(step):
    return [(i, i // 8 * 8 + (i // 2 + step) % 4 * 2 + i % 2) for i in range(16)]


def quarters():
    pairs = []
    for batch in range(Y_LO * Z):
        for seq in range(16):
            y_lo, z = divmod(batch, Z)
            y_hi, x = seq // 8, seq // 2 % 4
            source = (y_hi * Y_LO + y_lo + (0, 1, 2, -1)[x]) % (2 * Y_LO)
            source_batch = source % Y_LO * Z + z
            pairs.append((source_batch * 16 + source // Y_LO * 8 + seq % 8, batch * 16 + seq))
    return pairs


def to_all(values, axis, groups=None):
    count = len(groups[0]) if groups else lax.axis_size(axis)
    return lax.all_to_all(
        jnp.broadcast_to(values[None], (count,) + values.shape),
        axis, 0, 0, axis_index_groups=groups, tiled=True,
    )


def qkv_rows(gathered):
    tiles = gathered[:, :, 1920:].reshape(Z, 3, 8, 7, 128)
    return tiles.transpose(0, 3, 2, 1, 4).reshape(448, 384)


def attend_kernel(first_ref, r_ref, o_ref):
    keys = jnp.concatenate([r_ref[j, KEY : 2 * KEY, :] for j in range(16)], axis=1).T
    values = jnp.concatenate([r_ref[j, 2 * KEY :, :] for j in range(16)], axis=1)
    first = first_ref[0]
    for i in range(0, 8, 2):
        q = jnp.concatenate([r_ref[first + i, :KEY, :], r_ref[first + i + 1, :KEY, :]], axis=1)
        scores = jnp.dot(keys, q, preferred_element_type=jnp.float32)
        exps = jnp.exp(scores - jnp.max(scores, axis=0, keepdims=True))
        total = jnp.sum(exps, axis=0, keepdims=True)
        out = jnp.dot(values, exps.astype(jnp.bfloat16), preferred_element_type=jnp.float32)
        out = (out / total).astype(jnp.bfloat16)
        o_ref[i] = out[:, :128]
        o_ref[i + 1] = out[:, 128:]


def attend(first, received):
    return pl.pallas_call(
        attend_kernel,
        out_shape=jax.ShapeDtypeStruct((8, VAL, 128), jnp.bfloat16),
        in_specs=[
            pl.BlockSpec(memory_space=pltpu.SMEM),
            pl.BlockSpec(memory_space=pltpu.VMEM),
        ],
        out_specs=pl.BlockSpec(memory_space=pltpu.VMEM),
        compiler_params=pltpu.CompilerParams(vmem_limit_bytes=20 << 20),
        name="attend",
    )(first, received)


def conv_kernel(where_ref, x0, x1, x2, x3, sums_ref, norm_ref, mine_ref, other_ref, bias_ref,
                out_ref, act, product, *, count):
    core, x_at, y_hi = where_ref[0], where_ref[1], where_ref[2]
    bias = bias_ref[pl.ds(lax.rem(x_at + where_ref[3], 4), 1)]
    mean = sums_ref[0:1] / count
    scale = lax.rsqrt(sums_ref[1:2] / count - mean * mean + epsilon) * norm_ref[0:1]
    shift = norm_ref[1:2]
    near = pl.multiple_of(core * 384, 128)
    far = pl.multiple_of(384 - core * 384, 128)

    def activated(values):
        return jax.nn.gelu(
            (values.astype(jnp.float32) - mean) * scale + shift, approximate=True
        ).astype(jnp.bfloat16)

    for k, x_ref in enumerate((x0, x1, x2, x3)):
        slot = lax.rem(x_at + 4 - k, 4)
        seq = y_hi * 8 + slot * 2 + core
        edge = activated(x_ref[0:16])
        row = lax.broadcasted_iota(jnp.int32, edge.shape, 0)
        act[k, 0:16] = jnp.where((row >= 14) & (seq > 0), edge, jnp.zeros_like(edge))
        edge = activated(x_ref[272:288])
        act[k, 272:288] = jnp.where((row < 2) & (seq < 15), edge, jnp.zeros_like(edge))

        @pl.loop(1, 17)
        def _(i):
            rows = pl.ds(pl.multiple_of(i * 16, 16), 16)
            act[k, rows] = activated(x_ref[rows])

        for tap in range(5):
            nt = (((1,), (1,)), ((), ()))
            both = lax.dot_general(
                act[k, :, pl.ds(near, 384)], mine_ref[:, tap * 384 : (tap + 1) * 384], nt, preferred_element_type=jnp.float32
            ) + lax.dot_general(
                act[k, :, pl.ds(far, 384)], other_ref[:, tap * 384 : (tap + 1) * 384], nt, preferred_element_type=jnp.float32
            )
            product[tap] = both[:, :128]
            product[5 + tap, :, :64] = both[:, 128:]
        for base, lanes in ((0, 128), (5, 64)):
            pair = []
            for odd in range(2):
                total = product[base, pl.ds(14 + odd, 128, stride=2), :]
                for tap in range(1, 5):
                    total = total + product[base + tap, pl.ds(14 + odd + tap, 128, stride=2), :]
                pair.append(total[:, :lanes])
            columns = slice(base // 5 * 128, base // 5 * 128 + lanes)
            pooled = jnp.maximum(pair[0], pair[1]) + bias[:, columns]
            pooled = pooled.astype(jnp.bfloat16)
            if base == 0:
                out_ref[slot, :128] = pooled
            else:
                out_ref[slot, 128:, :64] = pooled[:64]
                out_ref[slot, 128:, 64:] = pooled[64:]


def conv_block(where, blocks, sums, norm, mine, other, bias, count):
    vmem = pl.BlockSpec(memory_space=pltpu.VMEM)
    return pl.pallas_call(
        functools.partial(conv_kernel, count=count),
        out_shape=jax.ShapeDtypeStruct((4, 192, 128), jnp.bfloat16),
        in_specs=[pl.BlockSpec(memory_space=pltpu.SMEM)] + [vmem] * 9,
        out_specs=vmem,
        scratch_shapes=[
            pltpu.VMEM((4, 288, 768), jnp.bfloat16),
            pltpu.VMEM((10, 288, 128), jnp.float32),
        ],
        compiler_params=pltpu.CompilerParams(vmem_limit_bytes=14 << 20),
        name="conv_block",
    )(where, *blocks, sums, norm, mine, other, bias)


def project_kernel(where_ref, part_ref, norm_ref, *refs):
    weights, (pooled_ref, out_ref, normed, proj) = refs[:6], refs[6:]
    core, x_at, y_lo = where_ref[0], where_ref[1], where_ref[3]
    near = pl.multiple_of(core * 384, 128)
    far = pl.multiple_of(384 - core * 384, 128)
    pieces = []
    for i in range(4):
        piece = part_ref[lax.rem(i + 4 - y_lo, 4)]
        pieces.append(piece[:128])
        pieces.append(jnp.concatenate([piece[128:, :64], piece[128:, 64:]], axis=0))
    pooled = jnp.concatenate(pieces, axis=1)
    pooled_ref[...] = pooled
    wide = pooled.astype(jnp.float32)
    wide = wide - jnp.mean(wide, axis=-1, keepdims=True)
    spread = jnp.mean(wide * wide, axis=-1, keepdims=True)
    normed[...] = (wide * lax.rsqrt(spread + epsilon) * norm_ref[0:1] + norm_ref[1:2]).astype(
        jnp.bfloat16
    )
    nt = (((1,), (1,)), ((), ()))
    for k in range(4):
        rows = pl.ds(pl.multiple_of(lax.rem(x_at + y_lo + 4 - k, 4) * 448, 64), 448)
        proj[rows] = lax.dot_general(
            weights[k][...], normed[:, pl.ds(near, 384)], nt,
            preferred_element_type=jnp.float32,
        ) + lax.dot_general(
            weights[4][...] if k == 0 else weights[5][(k - 1) * 448 : k * 448], normed[:, pl.ds(far, 384)], nt,
            preferred_element_type=jnp.float32,
        )
    for h in range(HEADS):
        q = (proj[h * KEY : (h + 1) * KEY] * KEY ** (-0.5)).astype(jnp.bfloat16)
        k = proj[512 + h * KEY : 512 + (h + 1) * KEY].astype(jnp.bfloat16)
        v = proj[1024 + h * VAL : 1024 + (h + 1) * VAL].astype(jnp.bfloat16)
        for d in (h, h + HEADS):
            out_ref[d, :KEY] = q
            out_ref[d, KEY : 2 * KEY] = k
            out_ref[d, 2 * KEY :] = v


def project(where, part, norm, weights):
    vmem = pl.BlockSpec(memory_space=pltpu.VMEM)
    return pl.pallas_call(
        project_kernel,
        out_shape=(
            jax.ShapeDtypeStruct((128, 768), jnp.bfloat16),
            jax.ShapeDtypeStruct((16, ROWS, 128), jnp.bfloat16),
        ),
        in_specs=[pl.BlockSpec(memory_space=pltpu.SMEM)] + [vmem] * 8,
        out_specs=(vmem, vmem),
        scratch_shapes=[
            pltpu.VMEM((128, 768), jnp.bfloat16),
            pltpu.VMEM((1792, 128), jnp.float32),
        ],
        compiler_params=pltpu.CompilerParams(vmem_limit_bytes=14 << 20),
        name="project",
    )(where, part, norm, *weights)


def on_device(
    sequence_input, bn_gain, bn_bias, conv_weight, conv_bias, ln_gain, ln_bias, qkv_weight
):
    raw = sequence_input[0]
    channels = raw.shape[1]
    y_lo = lax.axis_index("batch") // Z
    seq = lax.axis_index("seq")
    core, x_at = seq % 2, seq // 2 % 4
    where = jnp.stack([core, x_at, seq // 8, y_lo]).astype(jnp.int32)
    swap = [(i, i ^ 1) for i in range(16)]

    conv_half = lax.dynamic_slice(conv_weight.transpose(0, 2, 1), (0, 0, core * 384), (5, 24, 384))
    qkv_half = lax.dynamic_slice(qkv_weight.T, (0, core * 384), (56, 384))
    mine = jnp.concatenate(
        [
            conv_half.transpose(1, 0, 2).reshape(24, 1920),
            qkv_half.reshape(7, 8, 3, 128).transpose(2, 1, 0, 3).reshape(24, 896),
        ],
        axis=1,
    )
    mine = lax.ppermute(mine, ("batch", "seq"), quarters())

    pad = jnp.zeros((14, channels), raw.dtype)
    left = lax.ppermute(raw[-2:], "seq", [(i, i + 1) for i in range(15)])
    right = lax.ppermute(raw[:2], "seq", [(i + 1, i) for i in range(15)])
    block = jnp.concatenate([pad, left, raw, right, pad], axis=0)

    wide = raw.astype(jnp.float32)
    sums = jnp.stack([jnp.sum(wide, axis=0), jnp.sum(wide * wide, axis=0)])
    sums, mine, block = lax.optimization_barrier((sums, mine, block))
    mine = to_all(mine, "batch", Z_GROUPS)
    for bit in (1, 2, 4, 8):
        sums = sums + lax.ppermute(sums, "seq", [(i, i ^ bit) for i in range(16)])
    sums, block = lax.optimization_barrier((sums, block))
    blocks = [block] + [lax.ppermute(block, "seq", x_shift(k)) for k in range(1, 4)]
    sums, mine = lax.optimization_barrier((sums, mine))
    other = lax.ppermute(mine, "seq", swap)
    own = qkv_rows(mine)
    near = [lax.ppermute(own, "seq", x_shift(k)) for k in range(1, 4)]
    sums = jnp.sum(to_all(sums, "batch"), axis=0)
    count = float(raw.shape[0] * lax.axis_size("batch") * lax.axis_size("seq"))

    part = conv_block(
        where, blocks, sums, jnp.stack([bn_gain, bn_bias]), mine.reshape(192, 2816), other.reshape(192, 2816),
        conv_bias.reshape(4, 192), count,
    )
    near, other = lax.optimization_barrier((part, near, other))[1:]
    far = lax.ppermute(jnp.concatenate(near, axis=0), "seq", swap)
    weights = [own] + near + [qkv_rows(other), far]
    part = lax.all_to_all(part, "seq", 0, 0, axis_index_groups=X_GROUPS, tiled=True)
    pooled, packed = project(where, part, jnp.stack([ln_gain, ln_bias]), weights)
    packed = lax.all_to_all(packed, "seq", 0, 0, tiled=True)
    out = attend((seq // 8 * 8).astype(jnp.int32)[None], packed)
    out = lax.all_to_all(out, "seq", 0, 0, axis_index_groups=HALF_GROUPS, tiled=True)
    attended = out.reshape(HEADS * VAL, 128).T
    return (pooled[None], attended[None])


def solution(mesh):
    placed = (
        P("batch", "seq", None),
        P(),
        P(),
        P(None, None, "batch"),
        P(),
        P(),
        P(),
        P(None, "batch"),
    )
    return jax.shard_map(
        on_device,
        mesh=mesh,
        in_specs=placed,
        out_specs=(P("batch", "seq", None), P("batch", "seq", None)),
        check_vma=False,
    )
```

```python
import functools

import jax
import jax.numpy as jnp
from jax import lax
from jax.experimental import pallas as pl
from jax.experimental.pallas import tpu as pltpu
from jax.sharding import PartitionSpec as P

HEADS = 8
KEY = 64
VAL = 96
ROWS = 2 * KEY + VAL
epsilon = 1e-05

Y_LO, Z = 4, 8
Z_GROUPS = [[y * Z + z for z in range(Z)] for y in range(Y_LO)]
X_GROUPS = [[half * 8 + x * 2 + core for x in range(4)] for half in range(2) for core in range(2)]
HALF_GROUPS = [list(range(8)), list(range(8, 16))]


def x_shift(step):
    return [(i, i // 8 * 8 + (i // 2 + step) % 4 * 2 + i % 2) for i in range(16)]


def quarters():
    pairs = []
    for batch in range(Y_LO * Z):
        for seq in range(16):
            y_lo, z = divmod(batch, Z)
            y_hi, x = seq // 8, seq // 2 % 4
            source = (y_hi * Y_LO + y_lo + (0, 1, 2, -1)[x]) % (2 * Y_LO)
            source_batch = source % Y_LO * Z + z
            pairs.append((source_batch * 16 + source // Y_LO * 8 + seq % 8, batch * 16 + seq))
    return pairs


def to_all(values, axis, groups=None):
    count = len(groups[0]) if groups else lax.axis_size(axis)
    return lax.all_to_all(
        jnp.broadcast_to(values[None], (count,) + values.shape),
        axis, 0, 0, axis_index_groups=groups, tiled=True,
    )


def qkv_rows(gathered):
    tiles = gathered[:, :, 1920:].reshape(Z, 3, 8, 7, 128)
    return tiles.transpose(0, 3, 2, 1, 4).reshape(448, 384)


def attend_kernel(first_ref, r_ref, o_ref):
    keys = jnp.concatenate([r_ref[j, KEY : 2 * KEY, :] for j in range(16)], axis=1).T
    values = jnp.concatenate([r_ref[j, 2 * KEY :, :] for j in range(16)], axis=1)
    first = first_ref[0]
    for i in range(0, 8, 2):
        q = jnp.concatenate([r_ref[first + i, :KEY, :], r_ref[first + i + 1, :KEY, :]], axis=1)
        scores = jnp.dot(keys, q, preferred_element_type=jnp.float32)
        exps = jnp.exp(scores - jnp.max(scores, axis=0, keepdims=True))
        total = jnp.sum(exps, axis=0, keepdims=True)
        out = jnp.dot(values, exps.astype(jnp.bfloat16), preferred_element_type=jnp.float32)
        out = (out / total).astype(jnp.bfloat16)
        o_ref[i] = out[:, :128]
        o_ref[i + 1] = out[:, 128:]


def attend(first, received):
    return pl.pallas_call(
        attend_kernel,
        out_shape=jax.ShapeDtypeStruct((8, VAL, 128), jnp.bfloat16),
        in_specs=[
            pl.BlockSpec(memory_space=pltpu.SMEM),
            pl.BlockSpec(memory_space=pltpu.VMEM),
        ],
        out_specs=pl.BlockSpec(memory_space=pltpu.VMEM),
        compiler_params=pltpu.CompilerParams(vmem_limit_bytes=20 << 20),
        name="attend",
    )(first, received)


def conv_kernel(where_ref, x0, x1, x2, x3, sums_ref, norm_ref, mine_ref, other_ref, bias_ref,
                out_ref, act, product, *, count):
    core, x_at, y_hi = where_ref[0], where_ref[1], where_ref[2]
    bias = bias_ref[pl.ds(lax.rem(x_at + where_ref[3], 4), 1)]
    sums = jnp.sum(sums_ref[...], axis=0)
    mean = sums[0:1] / count
    scale = lax.rsqrt(sums[1:2] / count - mean * mean + epsilon) * norm_ref[0:1]
    shift = norm_ref[1:2]
    near = pl.multiple_of(core * 384, 128)
    far = pl.multiple_of(384 - core * 384, 128)

    def activated(values):
        return jax.nn.gelu(
            (values.astype(jnp.float32) - mean) * scale + shift, approximate=True
        ).astype(jnp.bfloat16)

    for k, x_ref in enumerate((x0, x1, x2, x3)):
        slot = lax.rem(x_at + 4 - k, 4)
        seq = y_hi * 8 + slot * 2 + core
        edge = activated(x_ref[0:16])
        row = lax.broadcasted_iota(jnp.int32, edge.shape, 0)
        act[k, 0:16] = jnp.where((row >= 14) & (seq > 0), edge, jnp.zeros_like(edge))
        edge = activated(x_ref[272:288])
        act[k, 272:288] = jnp.where((row < 2) & (seq < 15), edge, jnp.zeros_like(edge))

        @pl.loop(1, 17)
        def _(i):
            rows = pl.ds(pl.multiple_of(i * 16, 16), 16)
            act[k, rows] = activated(x_ref[rows])

        for tap in range(5):
            nt = (((1,), (1,)), ((), ()))
            both = lax.dot_general(
                act[k, :, pl.ds(near, 384)], mine_ref[:, tap * 384 : (tap + 1) * 384], nt, preferred_element_type=jnp.float32
            ) + lax.dot_general(
                act[k, :, pl.ds(far, 384)], other_ref[:, tap * 384 : (tap + 1) * 384], nt, preferred_element_type=jnp.float32
            )
            product[tap] = both[:, :128]
            product[5 + tap, :, :64] = both[:, 128:]
        for base, lanes in ((0, 128), (5, 64)):
            pair = []
            for odd in range(2):
                total = product[base, pl.ds(14 + odd, 128, stride=2), :]
                for tap in range(1, 5):
                    total = total + product[base + tap, pl.ds(14 + odd + tap, 128, stride=2), :]
                pair.append(total[:, :lanes])
            columns = slice(base // 5 * 128, base // 5 * 128 + lanes)
            pooled = jnp.maximum(pair[0], pair[1]) + bias[:, columns]
            pooled = pooled.astype(jnp.bfloat16)
            if base == 0:
                out_ref[slot, :128] = pooled
            else:
                out_ref[slot, 128:, :64] = pooled[:64]
                out_ref[slot, 128:, 64:] = pooled[64:]


def conv_block(where, blocks, sums, norm, mine, other, bias, count):
    vmem = pl.BlockSpec(memory_space=pltpu.VMEM)
    return pl.pallas_call(
        functools.partial(conv_kernel, count=count),
        out_shape=jax.ShapeDtypeStruct((4, 192, 128), jnp.bfloat16),
        in_specs=[pl.BlockSpec(memory_space=pltpu.SMEM)] + [vmem] * 9,
        out_specs=vmem,
        scratch_shapes=[
            pltpu.VMEM((4, 288, 768), jnp.bfloat16),
            pltpu.VMEM((10, 288, 128), jnp.float32),
        ],
        compiler_params=pltpu.CompilerParams(vmem_limit_bytes=14 << 20),
        name="conv_block",
    )(where, *blocks, sums, norm, mine, other, bias)


def project_kernel(where_ref, part_ref, norm_ref, *refs):
    weights, (pooled_ref, out_ref, normed, proj) = refs[:6], refs[6:]
    core, x_at, y_lo = where_ref[0], where_ref[1], where_ref[3]
    near = pl.multiple_of(core * 384, 128)
    far = pl.multiple_of(384 - core * 384, 128)
    pieces = []
    for i in range(4):
        piece = part_ref[lax.rem(i + 4 - y_lo, 4)]
        pieces.append(piece[:128])
        pieces.append(jnp.concatenate([piece[128:, :64], piece[128:, 64:]], axis=0))
    pooled = jnp.concatenate(pieces, axis=1)
    pooled_ref[...] = pooled
    wide = pooled.astype(jnp.float32)
    wide = wide - jnp.mean(wide, axis=-1, keepdims=True)
    spread = jnp.mean(wide * wide, axis=-1, keepdims=True)
    normed[...] = (wide * lax.rsqrt(spread + epsilon) * norm_ref[0:1] + norm_ref[1:2]).astype(
        jnp.bfloat16
    )
    nt = (((1,), (1,)), ((), ()))
    for k in range(4):
        rows = pl.ds(pl.multiple_of(lax.rem(x_at + y_lo + 4 - k, 4) * 448, 64), 448)
        proj[rows] = lax.dot_general(
            weights[k][...], normed[:, pl.ds(near, 384)], nt,
            preferred_element_type=jnp.float32,
        ) + lax.dot_general(
            weights[4][...] if k == 0 else weights[5][(k - 1) * 448 : k * 448], normed[:, pl.ds(far, 384)], nt,
            preferred_element_type=jnp.float32,
        )
    for h in range(HEADS):
        q = (proj[h * KEY : (h + 1) * KEY] * KEY ** (-0.5)).astype(jnp.bfloat16)
        k = proj[512 + h * KEY : 512 + (h + 1) * KEY].astype(jnp.bfloat16)
        v = proj[1024 + h * VAL : 1024 + (h + 1) * VAL].astype(jnp.bfloat16)
        for d in (h, h + HEADS):
            out_ref[d, :KEY] = q
            out_ref[d, KEY : 2 * KEY] = k
            out_ref[d, 2 * KEY :] = v


def project(where, part, norm, weights):
    vmem = pl.BlockSpec(memory_space=pltpu.VMEM)
    return pl.pallas_call(
        project_kernel,
        out_shape=(
            jax.ShapeDtypeStruct((128, 768), jnp.bfloat16),
            jax.ShapeDtypeStruct((16, ROWS, 128), jnp.bfloat16),
        ),
        in_specs=[pl.BlockSpec(memory_space=pltpu.SMEM)] + [vmem] * 8,
        out_specs=(vmem, vmem),
        scratch_shapes=[
            pltpu.VMEM((128, 768), jnp.bfloat16),
            pltpu.VMEM((1792, 128), jnp.float32),
        ],
        compiler_params=pltpu.CompilerParams(vmem_limit_bytes=14 << 20),
        name="project",
    )(where, part, norm, *weights)


def on_device(
    sequence_input, bn_gain, bn_bias, conv_weight, conv_bias, ln_gain, ln_bias, qkv_weight
):
    raw = sequence_input[0]
    channels = raw.shape[1]
    y_lo = lax.axis_index("batch") // Z
    seq = lax.axis_index("seq")
    core, x_at = seq % 2, seq // 2 % 4
    where = jnp.stack([core, x_at, seq // 8, y_lo]).astype(jnp.int32)
    swap = [(i, i ^ 1) for i in range(16)]

    conv_half = lax.dynamic_slice(conv_weight.transpose(0, 2, 1), (0, 0, core * 384), (5, 24, 384))
    qkv_half = lax.dynamic_slice(qkv_weight.T, (0, core * 384), (56, 384))
    mine = jnp.concatenate(
        [
            conv_half.transpose(1, 0, 2).reshape(24, 1920),
            qkv_half.reshape(7, 8, 3, 128).transpose(2, 1, 0, 3).reshape(24, 896),
        ],
        axis=1,
    )
    mine = lax.ppermute(mine, ("batch", "seq"), quarters())

    pad = jnp.zeros((14, channels), raw.dtype)
    left = lax.ppermute(raw[-2:], "seq", [(i, i + 1) for i in range(15)])
    right = lax.ppermute(raw[:2], "seq", [(i + 1, i) for i in range(15)])
    block = jnp.concatenate([pad, left, raw, right, pad], axis=0)

    wide = raw.astype(jnp.float32)
    sums = jnp.stack([jnp.sum(wide, axis=0), jnp.sum(wide * wide, axis=0)])
    sums, mine, block = lax.optimization_barrier((sums, mine, block))
    mine = to_all(mine, "batch", Z_GROUPS)
    for bit in (1, 2, 4, 8):
        sums = sums + lax.ppermute(sums, "seq", [(i, i ^ bit) for i in range(16)])
    sums, block = lax.optimization_barrier((sums, block))
    blocks = [block] + [lax.ppermute(block, "seq", x_shift(k)) for k in range(1, 4)]
    sums, mine = lax.optimization_barrier((sums, mine))
    other = lax.ppermute(mine, "seq", swap)
    own = qkv_rows(mine)
    near = [lax.ppermute(own, "seq", x_shift(k)) for k in range(1, 4)]
    sums = to_all(sums, "batch")
    count = float(raw.shape[0] * lax.axis_size("batch") * lax.axis_size("seq"))

    part = conv_block(
        where, blocks, sums, jnp.stack([bn_gain, bn_bias]), mine.reshape(192, 2816), other.reshape(192, 2816),
        conv_bias.reshape(4, 192), count,
    )
    near, other = lax.optimization_barrier((part, near, other))[1:]
    far = lax.ppermute(jnp.concatenate(near, axis=0), "seq", swap)
    weights = [own] + near + [qkv_rows(other), far]
    part = lax.all_to_all(part, "seq", 0, 0, axis_index_groups=X_GROUPS, tiled=True)
    pooled, packed = project(where, part, jnp.stack([ln_gain, ln_bias]), weights)
    packed = lax.all_to_all(packed, "seq", 0, 0, tiled=True)
    out = attend((seq // 8 * 8).astype(jnp.int32)[None], packed)
    out = lax.all_to_all(out, "seq", 0, 0, axis_index_groups=HALF_GROUPS, tiled=True)
    attended = out.reshape(HEADS * VAL, 128).T
    return (pooled[None], attended[None])


def solution(mesh):
    placed = (
        P("batch", "seq", None),
        P(),
        P(),
        P(None, None, "batch"),
        P(),
        P(),
        P(),
        P(None, "batch"),
    )
    return jax.shard_map(
        on_device,
        mesh=mesh,
        in_specs=placed,
        out_specs=(P("batch", "seq", None), P("batch", "seq", None)),
        check_vma=False,
    )
```
